32 devices in a mesh: site: 8 (over y, x, core), dp: 4 (over z).
Axes of the slice: x: 2, y: 2, z: 4, core: 2. Of those that a mesh axis runs over, the one named last changes fastest.
Arguments:
- inputs: bfloat16 [8, 12, 32, 4096], P('dp', None, None, 'site'), may hold values from -6 to 6
- cot_out: bfloat16 [8, 12, 32, 4096], P('dp', None, None, 'site'), may hold values from -18 to 18
- cot_skip: bfloat16 [8, 12, 256, 4096], P('dp', None, None, 'site'), may hold values from -6 to 6
- w_conv: bfloat16 [64, 64], replicated, may hold values from -0.75 to 0.75
- convolution_bias: float32 [64], replicated, may hold values from -3 to 3
- w_mix: bfloat16 [32, 96], replicated, may hold values from -0.625 to 0.625
- w_skip: bfloat16 [256, 32], replicated, may hold values from -1 to 1
- adj_cols: int32 [32, 4], P('site'), may hold values from 0 to 5, as said below
- used_block_count: int32 [32], P('site'), may hold values from 1 to 4, as said below
- adj_vals: bfloat16 [32, 4, 128, 128], P('site'), may hold values from -0.375 to 0.375
Outputs:
- grad_conv: float32 [64, 64], replicated
- grad_bias: float32 [64], replicated
- grad_mix: float32 [32, 96], replicated
- skip_weight_gradient: float32 [256, 32], replicated
- grad_inputs: bfloat16 [8, 12, 32, 4096], P('dp', None, None, 'site')
The draws below stay inside these ranges and needn't reach their ends.
Inputs may be any that keep to these rules, and one draw needn't show every extreme that they name: `adj_cols`: the 4 entries of a row are different column blocks of the partition's window. The first used_block_count entries of a row of adj_cols are used; every partition has a row block using all 4.
All inputs are finite; a program needn't handle non-finite values.
Results may differ from the reference program's by a relative error of at most 0.0057.
Values may be sent and summed in bfloat16 or wider, within the bound.
A program may use at most 64 MiB of HBM per device.

```python
import math
import jax
import jax.numpy as jnp
from jax import lax

C = 32
SKIP = 256
BLK = 128
KB = 4
TSTEP = 12
NB = 4
SITES = 4096
ROWBLOCKS = 32
BATCH = 8
N_SITE = 8


def draw_adj_cols(key, part):
    row_total = NB * N_SITE
    window_blocks = NB + 2
    scores = jax.random.randint(key, (row_total, window_blocks), 0, 1 << 20)
    scores = scores * window_blocks + jnp.arange(window_blocks, dtype=jnp.int32)[None, :]
    ranking = jnp.argsort(scores, axis=1)
    return ranking[:, :KB].astype(jnp.int32)


def draw_used_block_count(key, part):
    key_one, key_two = jax.random.split(key)
    counted = jax.random.randint(key_one, (N_SITE, NB), 1, KB + 1)
    full_slot = jax.random.randint(key_two, (N_SITE, 1), 0, NB)
    slot_index = jnp.arange(NB, dtype=jnp.int32)[None, :]
    return jnp.where(slot_index == full_slot, KB, counted).reshape(N_SITE * NB).astype(jnp.int32)


def draw_cot_out(key, part):
    full_shape = (BATCH, TSTEP, C, SITES)
    position = jnp.arange(SITES, dtype=jnp.float32) / float(SITES - 1)
    rising = jnp.exp(math.log(3.0) * position)
    values = jax.random.normal(key, full_shape, jnp.float32) * rising
    return jnp.clip(values, -18.0, 18.0).astype(jnp.bfloat16)


def block_levels(rng, extent, cuts, smallest, top_value):
    loudness, own = 1.0, jax.random.fold_in(rng, 6)
    for dim, shards_of in cuts:
        steps = jnp.exp(jax.random.uniform(jax.random.fold_in(own, dim), (shards_of,), jnp.float32, smallest / len(cuts), top_value / len(cuts)))
        loudness = loudness * jnp.repeat(steps, extent[dim] // shards_of).reshape([-1 if axis == dim else 1 for axis in range(len(extent))])
    return loudness


def gaussian(key, dims, deviation, most, cuts=(), kind=jnp.bfloat16):
    entries = jax.random.normal(key, dims, jnp.float32) * deviation
    if len(cuts) > 0:
        entries = block_levels(key, dims, cuts, -0.22, 0.18) * entries
    return jnp.clip(entries, min=-most, max=most).astype(kind)


def setup_inputs(seed: int = 0) -> dict:
    seeds = jax.random.split(jax.random.key(seed), 11)
    inputs = gaussian(seeds[0], (BATCH, TSTEP, C, SITES), 1.0, 6.0, ((0, 4), (3, 8)))
    cot_out = draw_cot_out(jax.random.fold_in(seeds[10], 71), 0)
    cot_skip = gaussian(seeds[2], (BATCH, TSTEP, SKIP, SITES), 1.0, 6.0, ((0, 4), (3, 8)))
    w_conv = gaussian(seeds[3], (2 * C, 2 * C), (2 * C) ** -0.5, 0.75)
    convolution_bias = gaussian(seeds[4], (2 * C,), 0.5, 3.0, (), jnp.float32)
    w_mix = gaussian(seeds[5], (C, 3 * C), (3 * C) ** -0.5, 0.625)
    w_skip = gaussian(seeds[6], (SKIP, C), C ** -0.5, 1.0)
    adj_cols = draw_adj_cols(jax.random.fold_in(seeds[10], 71), 0)
    used_block_count = draw_used_block_count(jax.random.fold_in(seeds[10], 71), 0)
    adj_vals = gaussian(seeds[9], (ROWBLOCKS, KB, BLK, BLK), (BLK * KB // 2) ** -0.5, 0.375, ((0, 8),))
    return {"inputs": inputs, "cot_out": cot_out, "cot_skip": cot_skip, "w_conv": w_conv, "convolution_bias": convolution_bias, "w_mix": w_mix, "w_skip": w_skip, "adj_cols": adj_cols, "used_block_count": used_block_count, "adj_vals": adj_vals}


def block_matrix(adj_cols, used_block_count, adj_vals):
    row_count, block_level_depth = adj_cols.shape
    blk_size = adj_vals.shape[-1]
    window_blocks = row_count + 2
    selected_blocks = adj_cols[:, :, None] == jnp.arange(window_blocks, dtype=jnp.int32)[None, None, :]
    alive_flags = jnp.arange(block_level_depth, dtype=jnp.int32)[None, :] < used_block_count[:, None]
    selection_mask = (selected_blocks & alive_flags[:, :, None]).astype(jnp.float32)
    blockwise = jnp.einsum("nkc,nkji->cjni", selection_mask, adj_vals.astype(jnp.float32))
    return blockwise.reshape(window_blocks * blk_size, row_count * blk_size).astype(jnp.bfloat16)


def hop_forward(field, matrix_list):
    n_rows = field.shape[0]
    pieces = field.reshape(n_rows, N_SITE, NB * BLK)
    before = jnp.roll(pieces, 1, axis=1)[:, :, -BLK:]
    after = jnp.roll(pieces, -1, axis=1)[:, :, :BLK]
    extended = jnp.concatenate([before, pieces, after], axis=2)
    result = jnp.einsum("mde,des->mds", extended.astype(jnp.float32), matrix_list.astype(jnp.float32))
    return result.reshape(n_rows, N_SITE * NB * BLK)


def hop_backward(grad_field, matrix_list):
    n_rows = grad_field.shape[0]
    pieces = grad_field.reshape(n_rows, N_SITE, NB * BLK)
    contrib = jnp.einsum("mds,des->mde", pieces.astype(jnp.float32), matrix_list.astype(jnp.float32))
    middle = contrib[:, :, BLK:-BLK]
    from_left = jnp.roll(contrib[:, :, -BLK:], 1, axis=1)
    from_right = jnp.roll(contrib[:, :, :BLK], -1, axis=1)
    middle = middle.at[:, :, :BLK].add(from_left)
    middle = middle.at[:, :, -BLK:].add(from_right)
    return middle.reshape(n_rows, N_SITE * NB * BLK)


def reference(inputs, cot_out, cot_skip, w_conv, convolution_bias, w_mix, w_skip, adj_cols, used_block_count, adj_vals):
    matrix_list = jax.vmap(block_matrix)(adj_cols.reshape(N_SITE, NB, KB), used_block_count.reshape(N_SITE, NB), adj_vals.reshape(N_SITE, NB, KB, BLK, BLK))
    channel_count = C
    convolution_forward = w_conv.astype(jnp.float32)
    mix_f = w_mix.astype(jnp.float32)
    skip_forward = w_skip.astype(jnp.float32)

    def one_window(window):
        feats, g_out, skip_gradient = window
        step_count = feats.shape[0]
        site_count = feats.shape[2]
        earlier = jnp.pad(feats[:-1], ((1, 0), (0, 0), (0, 0)))
        stacked_blocks = jnp.concatenate([earlier, feats], axis=1)
        preactivation = jnp.einsum("ul,elh->euh", convolution_forward, stacked_blocks.astype(jnp.float32)) + convolution_bias[None, :, None]
        filt = jnp.tanh(preactivation[:, :channel_count])
        gate = jax.nn.sigmoid(preactivation[:, channel_count:])
        hidden_state = (filt * gate).astype(jnp.bfloat16)
        n_rows = step_count * channel_count
        first_hop = hop_forward(hidden_state.reshape(n_rows, site_count), matrix_list).astype(jnp.bfloat16)
        second_hop = hop_forward(first_hop, matrix_list).astype(jnp.bfloat16)
        mixed_in = jnp.concatenate([hidden_state, first_hop.reshape(step_count, channel_count, site_count), second_hop.reshape(step_count, channel_count, site_count)], axis=1)
        grad_mix = jnp.einsum("tos,tjs->oj", g_out.astype(jnp.float32), mixed_in.astype(jnp.float32))
        skip_weight_gradient = jnp.einsum("nyl,nzl->yz", skip_gradient.astype(jnp.float32), hidden_state.astype(jnp.float32))
        mixing_backward = jnp.einsum("oj,tos->tjs", mix_f, g_out.astype(jnp.float32))
        grad_second = mixing_backward[:, 2 * channel_count:].astype(jnp.bfloat16).reshape(n_rows, site_count)
        first_hop_gradient = (mixing_backward[:, channel_count:2 * channel_count].reshape(n_rows, site_count) + hop_backward(grad_second, matrix_list)).astype(jnp.bfloat16)
        hidden_gradient = mixing_backward[:, :channel_count] + hop_backward(first_hop_gradient, matrix_list).reshape(step_count, channel_count, site_count) + jnp.einsum("ig,nif->ngf", skip_forward, skip_gradient.astype(jnp.float32))
        grad_pre = jnp.concatenate([hidden_gradient * gate * (1.0 - filt * filt), hidden_gradient * filt * gate * (1.0 - gate)], axis=1).astype(jnp.bfloat16)
        grad_conv = jnp.einsum("tos,tis->oi", grad_pre.astype(jnp.float32), stacked_blocks.astype(jnp.float32))
        grad_bias = jnp.sum(grad_pre.astype(jnp.float32), axis=(0, 2))
        back_in = jnp.einsum("oi,tos->tis", convolution_forward, grad_pre.astype(jnp.float32))
        grad_inputs = back_in[:, channel_count:] + jnp.pad(back_in[1:, :channel_count], ((0, 1), (0, 0), (0, 0)))
        return grad_conv, grad_bias, grad_mix, skip_weight_gradient, grad_inputs.astype(jnp.bfloat16)

    grad_conv, grad_bias, grad_mix, skip_weight_gradient, grad_inputs = lax.map(one_window, (inputs, cot_out, cot_skip))
    return (jnp.sum(grad_conv, axis=0), jnp.sum(grad_bias, axis=0), jnp.sum(grad_mix, axis=0), jnp.sum(skip_weight_gradient, axis=0), grad_inputs)
```

```python
import functools

import jax
import jax.numpy as jnp
from jax import lax
from jax.experimental import pallas as pl
from jax.experimental.pallas import tpu as pltpu
from jax.sharding import PartitionSpec as P

BLK = 128
GROUP = 8
MESH = pl.DeviceIdType.MESH
F32 = jnp.float32
BF16 = jnp.bfloat16


def mm(a, b):
    return jnp.dot(a, b, preferred_element_type=F32)


def nt(a, b):
    return lax.dot_general(a, b, (((1,), (1,)), ((), ())), preferred_element_type=F32)


def loop(n, f):
    def step(i, carry):
        f(i)
        return carry

    lax.fori_loop(0, n, step, 0)


def kernel(
    cfg,
    x_ref, co_ref, cs_ref, wc_ref, bias_ref, wm_ref, ws_ref, cols_ref, cnt_ref, adj_ref,
    out_conv, out_bias, out_mix, out_skip, out_gi,
    xm, xh, co, cs, av, a_mid, a_bnd, wct, wmt, wst, bcol,
    g2, c1, send_c, recv_c, fb, sg, mx, hh, f1h, gh, gp, gi,
    gs_acc, gm_acc, gc_acc, gb_acc, pack, rs_buf, dp_buf, fin,
    sem_loc, sem_cs, sem_out, e_send, e_recv, r_send, r_recv, d_send, d_recv, a_send, a_recv,
):
    n_site, n_dp, n_b, n_t, C, S, K, ct = cfg
    per_b = n_t // ct
    n_ch = n_b * per_b
    rows = ct * C
    nb = S // BLK
    site = lax.axis_index("site")
    dp = lax.axis_index("dp")
    right = lax.rem(site + 1, n_site)
    left = lax.rem(site + n_site - 1, n_site)
    n_q = (n_site // GROUP) * n_dp
    base = (site // GROUP) * GROUP
    loc = lax.rem(site, GROUP)
    q = (site // GROUP) * n_dp + dp

    def group_peer(j):
        return base + lax.rem(loc + j, GROUP)

    def cross_peer(j):
        other = lax.rem(q + j, n_q)
        return {"site": (other // n_dp) * GROUP + loc, "dp": lax.rem(other, n_dp)}

    barrier = pltpu.get_barrier_semaphore()
    signals = 0
    if n_site > GROUP:
        for p in (left, right):
            pl.semaphore_signal(barrier, inc=1, device_id={"site": p}, device_id_type=MESH)
            signals += 1
    for j in range(1, GROUP):
        pl.semaphore_signal(barrier, inc=1, device_id={"site": group_peer(j)}, device_id_type=MESH)
        signals += 1
    for j in range(1, n_q):
        pl.semaphore_signal(barrier, inc=1, device_id=cross_peer(j), device_id_type=MESH)
        signals += 1

    ld_adj = pltpu.make_async_copy(adj_ref, av, sem_loc.at[0])
    ld_co = pltpu.make_async_copy(co_ref, co, sem_loc.at[1])
    ld_x = pltpu.make_async_copy(x_ref, xm.at[:, 1:], sem_loc.at[2])
    ld_adj.start()
    ld_co.start()
    ld_x.start()

    def ld_cs(ch):
        r = pl.ds(ch * ct, ct)
        return pltpu.make_async_copy(cs_ref.at[r], cs.at[r], sem_cs.at[ch])

    for ch in range(n_ch):
        ld_cs(ch).start()

    wct[...] = wc_ref[...].astype(F32).T.astype(BF16)
    wmt[...] = wm_ref[...].astype(F32).T.astype(BF16)
    wst[...] = ws_ref[...].astype(F32).T.astype(BF16)
    bcol[...] = jnp.broadcast_to(bias_ref[...], (BLK, 2 * C)).T
    for b in range(n_b):
        xm[b, 0] = jnp.zeros((C, S), BF16)
        xh[b, 0] = jnp.zeros((C, 2 * BLK), BF16)
        gp[b, n_t] = jnp.zeros((2 * C, S), BF16)

    pl.semaphore_wait(barrier, signals)

    def remote(src, dst, e, side, ch, target):
        return pltpu.make_async_remote_copy(
            src_ref=src, dst_ref=dst, send_sem=e_send.at[e, side, ch],
            recv_sem=e_recv.at[e, side, ch], device_id={"site": target}, device_id_type=MESH,
        )

    lo, hi = pl.ds(0, BLK), pl.ds(S - BLK, BLK)
    h_lo, h_hi = pl.ds(0, BLK), pl.ds(BLK, BLK)

    def ex_x(ch):
        b, t0 = ch // per_b, lax.rem(ch, per_b) * ct
        src = x_ref.at[b, pl.ds(t0, ct)]
        dst = xh.at[b, pl.ds(t0 + 1, ct)]
        return (
            remote(src.at[:, :, hi], dst.at[:, :, h_lo], 0, 0, ch, right),
            remote(src.at[:, :, lo], dst.at[:, :, h_hi], 0, 1, ch, left),
        )

    def ex_c(which):
        def make(ch):
            r = pl.ds(ch * ct, ct)
            return (
                remote(send_c.at[which, 1, r], recv_c.at[which, 0, r], 1 + which, 0, ch, right),
                remote(send_c.at[which, 0, r], recv_c.at[which, 1, r], 1 + which, 1, ch, left),
            )

        return make

    def ex_f(ch):
        r = pl.ds(ch * ct, ct)
        src = mx.at[r, pl.ds(C, C)]
        dst = f1h.at[r]
        return (
            remote(src.at[:, :, hi], dst.at[:, :, h_lo], 3, 0, ch, right),
            remote(src.at[:, :, lo], dst.at[:, :, h_hi], 3, 1, ch, left),
        )

    def start(pair):
        for p in pair:
            p.start()

    def arrived(pair):
        for p in pair:
            p.wait_recv()

    for ch in range(n_ch):
        start(ex_x(ch))

    ld_adj.wait()
    for c in range(nb + 2):
        for r in range(nb):
            acc = jnp.zeros((BLK, BLK), F32)
            for k in range(K):
                on = jnp.where(
                    jnp.logical_and(cols_ref[r, k] == c, k < cnt_ref[r]), F32(1.0), F32(0.0)
                )
                acc = acc + av[r, k].astype(F32) * on
            blk = acc.astype(BF16)
            if c == 0 or c == nb + 1:
                o = 0 if c == 0 else BLK
                a_bnd[o : o + BLK, r * BLK : (r + 1) * BLK] = blk
            else:
                a_mid[(c - 1) * BLK : c * BLK, r * BLK : (r + 1) * BLK] = blk

    ld_co.wait()

    def back_one(ch):
        r = pl.ds(ch * ct, ct)
        for u in range(ct):
            t = ch * ct + u
            bm = mm(wmt[C:, :], co[t])
            c1[t] = bm[:C]
            g2[t] = bm[C:].astype(BF16)
        g = g2[r].reshape(rows, S)
        edge = nt(g, a_bnd[...]).astype(BF16).reshape(ct, C, 2 * BLK)
        send_c[0, 0, r] = edge[:, :, :BLK]
        send_c[0, 1, r] = edge[:, :, BLK:]
        start(ex_c(0)(ch))
        c1[r] = c1[r] + nt(g, a_mid[...]).reshape(ct, C, S)

    loop(n_ch, back_one)

    ld_x.wait()

    def forward_one(ch):
        b, t0 = ch // per_b, lax.rem(ch, per_b) * ct
        r = pl.ds(ch * ct, ct)
        arrived(ex_x(ch))
        for u in range(ct):
            t = ch * ct + u
            for src, width in ((xm, S), (xh, 2 * BLK)):
                st = src[b, pl.ds(t0 + u, 2)].reshape(2 * C, width)
                pre = mm(wc_ref[...], st) + bcol[:, 0:1]
                f = jnp.tanh(pre[:C])
                s = 0.5 * jnp.tanh(0.5 * pre[C:]) + 0.5
                h = (f * s).astype(BF16)
                if src is xm:
                    fb[t] = f
                    sg[t] = s
                    mx[t, 0:C] = h
                else:
                    hh[t] = h
        a = mx[r, 0:C].reshape(rows, S)
        f1 = mm(a, a_mid[...]) + mm(hh[r].reshape(rows, 2 * BLK), a_bnd[...])
        mx[r, C : 2 * C] = f1.astype(BF16).reshape(ct, C, S)
        start(ex_f(ch))

    loop(n_ch, forward_one)

    def back_two(ch):
        r = pl.ds(ch * ct, ct)
        arrived(ex_c(0)(ch))
        c1[r, :, lo] = c1[r, :, lo] + recv_c[0, 0, r].astype(F32)
        c1[r, :, hi] = c1[r, :, hi] + recv_c[0, 1, r].astype(F32)
        g = c1[r].astype(BF16).reshape(rows, S)
        edge = nt(g, a_bnd[...]).astype(BF16).reshape(ct, C, 2 * BLK)
        send_c[1, 0, r] = edge[:, :, :BLK]
        send_c[1, 1, r] = edge[:, :, BLK:]
        start(ex_c(1)(ch))
        gh[r] = nt(g, a_mid[...]).reshape(ct, C, S)

    loop(n_ch, back_two)

    gs_acc[...] = jnp.zeros_like(gs_acc)
    gm_acc[...] = jnp.zeros_like(gm_acc)
    gc_acc[...] = jnp.zeros_like(gc_acc)
    gb_acc[...] = jnp.zeros_like(gb_acc)

    def skip(ch):
        ld_cs(ch).wait()
        tot = gs_acc[...]
        for u in range(ct):
            t = ch * ct + u
            tot = tot + nt(mx[t, 0:C], cs[t])
            gh[t] = gh[t] + mm(wst[...], cs[t]) + mm(wmt[:C, :], co[t])
        gs_acc[...] = tot

    loop(n_ch, skip)

    def forward_two(ch):
        r = pl.ds(ch * ct, ct)
        arrived(ex_f(ch))
        f1 = mx[r, C : 2 * C].reshape(rows, S)
        f2 = mm(f1, a_mid[...]) + mm(f1h[r].reshape(rows, 2 * BLK), a_bnd[...])
        mx[r, 2 * C :] = f2.astype(BF16).reshape(ct, C, S)
        tot = gm_acc[:, : 3 * C]
        for u in range(ct):
            t = ch * ct + u
            tot = tot + nt(co[t], mx[t])
        gm_acc[:, : 3 * C] = tot

    loop(n_ch, forward_two)

    def finish(ch):
        b, t0 = ch // per_b, lax.rem(ch, per_b) * ct
        r = pl.ds(ch * ct, ct)
        arrived(ex_c(1)(ch))
        gh[r, :, lo] = gh[r, :, lo] + recv_c[1, 0, r].astype(F32)
        gh[r, :, hi] = gh[r, :, hi] + recv_c[1, 1, r].astype(F32)
        tot = gc_acc[:, : 2 * C]
        tob = gb_acc[...]
        for u in range(ct):
            t = ch * ct + u
            g, f, s = gh[t], fb[t], sg[t]
            gs = g * s
            v = jnp.concatenate([gs * (1.0 - f * f), gs * f * (1.0 - s)], axis=0).astype(BF16)
            gp[b, t0 + u] = v
            w = v.astype(F32)
            for m in range(nb):
                tob = tob + w[:, m * BLK : (m + 1) * BLK]
            tot = tot + nt(v, xm[b, pl.ds(t0 + u, 2)].reshape(2 * C, S))
        gc_acc[:, : 2 * C] = tot
        gb_acc[...] = tob

    loop(n_ch, finish)

    pack[:, 16:24, :] = jnp.zeros((GROUP, 8, BLK), F32)
    lane = lax.broadcasted_iota(jnp.int32, (2 * C, BLK), 1)
    both = jnp.where(lane < 2 * C, gc_acc[...], jnp.sum(gb_acc[...], axis=1, keepdims=True))
    for i in range(GROUP):
        o = 8 * (i % 4)
        p = BLK * (i // 4)
        pack[i, 0:8] = gs_acc[o : o + 8, p : p + BLK]
        pack[i, 8:16] = both[8 * i : 8 * i + 8]
        pack[i, 16:20] = gm_acc[4 * i : 4 * i + 4]

    def rs(j):
        peer = lax.rem(loc + j, GROUP)
        return pltpu.make_async_remote_copy(
            src_ref=pack.at[peer], dst_ref=rs_buf.at[j], send_sem=r_send.at[j],
            recv_sem=r_recv.at[j], device_id={"site": base + peer}, device_id_type=MESH,
        )

    def cross(j):
        return pltpu.make_async_remote_copy(
            src_ref=dp_buf.at[q], dst_ref=dp_buf.at[q], send_sem=d_send.at[j],
            recv_sem=d_recv.at[j], device_id=cross_peer(j), device_id_type=MESH,
        )

    def gather(j):
        return pltpu.make_async_remote_copy(
            src_ref=fin.at[loc], dst_ref=fin.at[loc], send_sem=a_send.at[j],
            recv_sem=a_recv.at[j], device_id={"site": group_peer(j)}, device_id_type=MESH,
        )

    for j in range(1, GROUP):
        rs(j).start()

    wct_now, wct_old = wct[C:, :], wct[:C, :]

    def inputs_grad(ch):
        b, t0 = ch // per_b, lax.rem(ch, per_b) * ct
        r = pl.ds(ch * ct, ct)
        for u in range(ct):
            v = mm(wct_now, gp[b, t0 + u]) + mm(wct_old, gp[b, t0 + u + 1])
            gi[ch * ct + u] = v.astype(BF16)
        pltpu.make_async_copy(gi.at[r], out_gi.at[b, pl.ds(t0, ct)], sem_out.at[ch]).start()

    loop(n_ch, inputs_grad)

    total = pack[loc]
    for j in range(1, GROUP):
        rs(j).wait_recv()
        total = total + rs_buf[j]
    dp_buf[q] = total
    for j in range(1, n_q):
        cross(j).start()
    for j in range(1, n_q):
        cross(j).wait_recv()
    total = dp_buf[0]
    for i in range(1, n_q):
        total = total + dp_buf[i]
    fin[loc] = total
    for j in range(1, GROUP):
        gather(j).start()
    for j in range(1, GROUP):
        gather(j).wait_recv()

    for h in range(2):
        out_skip[h * BLK : (h + 1) * BLK, :] = fin[4 * h : 4 * h + 4, 0:8].reshape(C, BLK).T
    both = fin[:, 8:16].reshape(2 * C, BLK)
    out_conv[...] = both[:, : 2 * C]
    out_bias[...] = both.T[2 * C : 2 * C + 1, :]
    for i in range(GROUP):
        out_mix[4 * i : 4 * i + 4, :] = fin[i, 16:20, : 3 * C]

    for ch in range(n_ch):
        for make in (ex_x, ex_c(0), ex_c(1), ex_f):
            for p in make(ch):
                p.wait_send()
        b, t0 = ch // per_b, (ch % per_b) * ct
        pltpu.make_async_copy(
            gi.at[pl.ds(ch * ct, ct)], out_gi.at[b, pl.ds(t0, ct)], sem_out.at[ch]
        ).wait()
    for j in range(1, GROUP):
        rs(j).wait_send()
        gather(j).wait_send()
    for j in range(1, n_q):
        cross(j).wait_send()


def shards(mesh_shape, x, co, cs, wc, bias, wm, ws, cols, cnt, adj):
    n_site, n_dp = mesh_shape
    n_b, n_t, C, S = x.shape
    K = cols.shape[1]
    skip = cs.shape[2]
    ct = 6
    n_ch = n_b * n_t // ct
    n = n_b * n_t
    n_q = (n_site // GROUP) * n_dp
    cfg = (n_site, n_dp, n_b, n_t, C, S, K, ct)
    vm = pl.BlockSpec(memory_space=pltpu.VMEM)
    sm = pl.BlockSpec(memory_space=pltpu.SMEM)
    anys = pl.BlockSpec(memory_space=pl.ANY)
    V = pltpu.VMEM
    D = pltpu.SemaphoreType.DMA
    scratch = [
        V((n_b, n_t + 1, C, S), BF16),
        V((n_b, n_t + 1, C, 2 * BLK), BF16),
        V((n, C, S), BF16),
        V((n, skip, S), BF16),
        V(adj.shape, BF16),
        V((S, S), BF16),
        V((2 * BLK, S), BF16),
        V((2 * C, 2 * C), BF16),
        V((3 * C, C), BF16),
        V((C, skip), BF16),
        V((2 * C, BLK), F32),
        V((n, C, S), BF16),
        V((n, C, S), F32),
        V((2, 2, n, C, BLK), BF16),
        V((2, 2, n, C, BLK), BF16),
        V((n, C, S), F32),
        V((n, C, S), F32),
        V((n, 3 * C, S), BF16),
        V((n, C, 2 * BLK), BF16),
        V((n, C, 2 * BLK), BF16),
        V((n, C, S), F32),
        V((n_b, n_t + 1, 2 * C, S), BF16),
        V((n, C, S), BF16),
        V((C, skip), F32),
        V((C, BLK), F32),
        V((2 * C, BLK), F32),
        V((2 * C, BLK), F32),
        V((GROUP, 24, BLK), F32),
        V((GROUP, 24, BLK), F32),
        V((n_q, 24, BLK), F32),
        V((GROUP, 24, BLK), F32),
        D((3,)),
        D((n_ch,)),
        D((n_ch,)),
        D((4, 2, n_ch)),
        D((4, 2, n_ch)),
        D((GROUP,)),
        D((GROUP,)),
        D((n_q,)),
        D((n_q,)),
        D((GROUP,)),
        D((GROUP,)),
    ]
    conv, gb, mix, gskip, gin = pl.pallas_call(
        functools.partial(kernel, cfg),
        out_shape=(
            jax.ShapeDtypeStruct((2 * C, 2 * C), F32),
            jax.ShapeDtypeStruct((1, 2 * C), F32),
            jax.ShapeDtypeStruct((C, 3 * C), F32),
            jax.ShapeDtypeStruct((skip, C), F32),
            jax.ShapeDtypeStruct(x.shape, BF16),
        ),
        in_specs=[anys, anys, anys, vm, vm, vm, vm, sm, sm, anys],
        out_specs=(vm, vm, vm, vm, anys),
        scratch_shapes=scratch,
        compiler_params=pltpu.CompilerParams(
            collective_id=0, has_side_effects=True, vmem_limit_bytes=60 * 1024 * 1024
        ),
        name="layer",
    )(x, co.reshape(n, C, S), cs.reshape(n, skip, S), wc, bias.reshape(1, -1), wm, ws, cols, cnt, adj)
    return conv, gb.reshape(-1), mix, gskip, gin


def solution(mesh):
    placed = (
        P("dp", None, None, "site"),
        P("dp", None, None, "site"),
        P("dp", None, None, "site"),
        P(),
        P(),
        P(),
        P(),
        P("site", None),
        P("site"),
        P("site", None, None, None),
    )
    return jax.shard_map(
        functools.partial(shards, (mesh.shape["site"], mesh.shape["dp"])),
        mesh=mesh,
        in_specs=placed,
        out_specs=(P(), P(), P(), P(), P("dp", None, None, "site")),
        check_vma=False,
    )
```

```python
import functools

import jax
import jax.numpy as jnp
from jax import lax
from jax.experimental import pallas as pl
from jax.experimental.pallas import tpu as pltpu
from jax.sharding import PartitionSpec as P

BLK = 128
GROUP = 8
VMEM_LIMIT = 40 * 1024 * 1024
MESH = pl.DeviceIdType.MESH
F32 = jnp.float32
BF16 = jnp.bfloat16


def mm(a, b):
    return jnp.dot(a, b, preferred_element_type=F32)


def nt(a, b):
    return lax.dot_general(a, b, (((1,), (1,)), ((), ())), preferred_element_type=F32)


def loop(n, f):
    def step(i, carry):
        f(i)
        return carry

    lax.fori_loop(0, n, step, 0)


def kernel(
    cfg,
    x_ref, co_ref, cs_ref, wc_hbm, bias_hbm, wm_hbm, ws_hbm, cols_hbm, cnt_hbm, adj_ref,
    fin, gi,
    xm, xh, co, cs, av, a_mid, a_bnd, wct, wmt, bcol,
    g2, c1, send_c, recv_c, fb, sg, mx, hh, f1h, gh, gp,
    gs_acc, gm_acc, gc_acc, gb_acc, pack, rs_buf, dp_buf, got,
    wc_ref, bias_ref, wm_ref, ws_ref, cols_ref, cnt_ref, sem_small,
    sem_loc, sem_cs, e_send, e_recv, r_send, r_recv, d_send, d_recv, a_send, a_recv,
):
    n_site, n_dp, n_b, n_t, C, S, K, ct = cfg
    per_b = n_t // ct
    n_ch = n_b * per_b
    rows = ct * C
    nb = S // BLK
    site = lax.axis_index("site")
    dp = lax.axis_index("dp")
    right = lax.rem(site + 1, n_site)
    left = lax.rem(site + n_site - 1, n_site)
    n_q = (n_site // GROUP) * n_dp
    base = (site // GROUP) * GROUP
    loc = lax.rem(site, GROUP)
    q = (site // GROUP) * n_dp + dp

    def group_peer(j):
        return base + lax.rem(loc + j, GROUP)

    def cross_peer(j):
        other = lax.rem(q + j, n_q)
        return {"site": (other // n_dp) * GROUP + loc, "dp": lax.rem(other, n_dp)}

    barrier = pltpu.get_barrier_semaphore()
    signals = 0
    if n_site > GROUP:
        for p in (left, right):
            pl.semaphore_signal(barrier, inc=1, device_id={"site": p}, device_id_type=MESH)
            signals += 1
    for j in range(1, GROUP):
        pl.semaphore_signal(barrier, inc=1, device_id={"site": group_peer(j)}, device_id_type=MESH)
        signals += 1
    for j in range(1, n_q):
        pl.semaphore_signal(barrier, inc=1, device_id=cross_peer(j), device_id_type=MESH)
        signals += 1

    small = [
        pltpu.make_async_copy(src, dst, sem_small.at[i])
        for i, (src, dst) in enumerate(
            (
                (cols_hbm, cols_ref), (cnt_hbm, cnt_ref), (wm_hbm, wm_ref), (wc_hbm, wc_ref),
                (bias_hbm, bias_ref), (ws_hbm, ws_ref),
            )
        )
    ]
    for cp in small:
        cp.start()
    ld_adj = pltpu.make_async_copy(adj_ref, av, sem_loc.at[0])
    ld_co = pltpu.make_async_copy(co_ref, co, sem_loc.at[1])
    ld_x = pltpu.make_async_copy(x_ref, xm.at[:, 1:], sem_loc.at[2])
    ld_adj.start()
    ld_co.start()
    ld_x.start()

    def ld_cs(ch):
        r = pl.ds(ch * ct, ct)
        return pltpu.make_async_copy(cs_ref.at[r], cs.at[r], sem_cs.at[ch])

    for ch in range(n_ch):
        ld_cs(ch).start()

    for cp in small:
        cp.wait()
    wct[...] = wc_ref[...].astype(F32).T.astype(BF16)
    wmt[...] = wm_ref[...].astype(F32).T.astype(BF16)
    bcol[...] = jnp.broadcast_to(bias_ref[...], (BLK, 2 * C)).T
    for b in range(n_b):
        xm[b, 0] = jnp.zeros((C, S), BF16)
        xh[b, 0] = jnp.zeros((C, 2 * BLK), BF16)
        gp[b, n_t] = jnp.zeros((2 * C, S), BF16)

    pl.semaphore_wait(barrier, signals)

    def remote(src, dst, e, side, ch, target):
        return pltpu.make_async_remote_copy(
            src_ref=src, dst_ref=dst, send_sem=e_send.at[e, side, ch],
            recv_sem=e_recv.at[e, side, ch], device_id={"site": target}, device_id_type=MESH,
        )

    lo, hi = pl.ds(0, BLK), pl.ds(S - BLK, BLK)
    h_lo, h_hi = pl.ds(0, BLK), pl.ds(BLK, BLK)

    def ex_x(ch):
        b, t0 = ch // per_b, lax.rem(ch, per_b) * ct
        src = x_ref.at[b, pl.ds(t0, ct)]
        dst = xh.at[b, pl.ds(t0 + 1, ct)]
        return (
            remote(src.at[:, :, hi], dst.at[:, :, h_lo], 0, 0, ch, right),
            remote(src.at[:, :, lo], dst.at[:, :, h_hi], 0, 1, ch, left),
        )

    def ex_c(which):
        def make(ch):
            r = pl.ds(ch * ct, ct)
            return (
                remote(send_c.at[which, 1, r], recv_c.at[which, 0, r], 1 + which, 0, ch, right),
                remote(send_c.at[which, 0, r], recv_c.at[which, 1, r], 1 + which, 1, ch, left),
            )

        return make

    def ex_f(ch):
        r = pl.ds(ch * ct, ct)
        src = mx.at[r, pl.ds(C, C)]
        dst = f1h.at[r]
        return (
            remote(src.at[:, :, hi], dst.at[:, :, h_lo], 3, 0, ch, right),
            remote(src.at[:, :, lo], dst.at[:, :, h_hi], 3, 1, ch, left),
        )

    def start(pair):
        for p in pair:
            p.start()

    def arrived(pair):
        for p in pair:
            p.wait_recv()

    for ch in range(n_ch):
        start(ex_x(ch))

    ld_adj.wait()
    for c in range(nb + 2):
        for r in range(nb):
            acc = jnp.zeros((BLK, BLK), F32)
            for k in range(K):
                on = jnp.where(
                    jnp.logical_and(cols_ref[r, k] == c, k < cnt_ref[r]), F32(1.0), F32(0.0)
                )
                acc = acc + av[r, k].astype(F32) * on
            blk = acc.astype(BF16)
            if c == 0 or c == nb + 1:
                o = 0 if c == 0 else BLK
                a_bnd[o : o + BLK, r * BLK : (r + 1) * BLK] = blk
            else:
                a_mid[(c - 1) * BLK : c * BLK, r * BLK : (r + 1) * BLK] = blk

    ld_co.wait()

    def back_one(ch):
        r = pl.ds(ch * ct, ct)
        for u in range(ct):
            t = ch * ct + u
            bm = mm(wmt[C:, :], co[t])
            c1[t] = bm[:C]
            g2[t] = bm[C:].astype(BF16)
        g = g2[r].reshape(rows, S)
        edge = nt(g, a_bnd[...]).astype(BF16).reshape(ct, C, 2 * BLK)
        send_c[0, 0, r] = edge[:, :, :BLK]
        send_c[0, 1, r] = edge[:, :, BLK:]
        start(ex_c(0)(ch))
        c1[r] = c1[r] + nt(g, a_mid[...]).reshape(ct, C, S)

    loop(n_ch, back_one)

    ld_x.wait()

    def forward_one(ch):
        b, t0 = ch // per_b, lax.rem(ch, per_b) * ct
        r = pl.ds(ch * ct, ct)
        arrived(ex_x(ch))
        for u in range(ct):
            t = ch * ct + u
            for src, width in ((xm, S), (xh, 2 * BLK)):
                st = src[b, pl.ds(t0 + u, 2)].reshape(2 * C, width)
                pre = mm(wc_ref[...], st) + bcol[:, 0:1]
                f = jnp.tanh(pre[:C])
                s = 0.5 * jnp.tanh(0.5 * pre[C:]) + 0.5
                h = (f * s).astype(BF16)
                if src is xm:
                    fb[t] = f
                    sg[t] = s
                    mx[t, 0:C] = h
                else:
                    hh[t] = h
        a = mx[r, 0:C].reshape(rows, S)
        f1 = mm(a, a_mid[...]) + mm(hh[r].reshape(rows, 2 * BLK), a_bnd[...])
        mx[r, C : 2 * C] = f1.astype(BF16).reshape(ct, C, S)
        start(ex_f(ch))

    loop(n_ch, forward_one)

    def back_two(ch):
        r = pl.ds(ch * ct, ct)
        arrived(ex_c(0)(ch))
        c1[r, :, lo] = c1[r, :, lo] + recv_c[0, 0, r].astype(F32)
        c1[r, :, hi] = c1[r, :, hi] + recv_c[0, 1, r].astype(F32)
        g = c1[r].astype(BF16).reshape(rows, S)
        edge = nt(g, a_bnd[...]).astype(BF16).reshape(ct, C, 2 * BLK)
        send_c[1, 0, r] = edge[:, :, :BLK]
        send_c[1, 1, r] = edge[:, :, BLK:]
        start(ex_c(1)(ch))
        gh[r] = nt(g, a_mid[...]).reshape(ct, C, S)

    loop(n_ch, back_two)

    gs_acc[...] = jnp.zeros_like(gs_acc)
    gm_acc[...] = jnp.zeros_like(gm_acc)
    gc_acc[...] = jnp.zeros_like(gc_acc)
    gb_acc[...] = jnp.zeros_like(gb_acc)

    def skip(ch):
        ld_cs(ch).wait()
        tot = gs_acc[...]
        for u in range(ct):
            t = ch * ct + u
            tot = tot + nt(mx[t, 0:C], cs[t])
            gh[t] = gh[t] + mm(ws_ref[...], cs[t]) + mm(wmt[:C, :], co[t])
        gs_acc[...] = tot

    loop(n_ch, skip)

    def forward_two(ch):
        r = pl.ds(ch * ct, ct)
        arrived(ex_f(ch))
        f1 = mx[r, C : 2 * C].reshape(rows, S)
        f2 = mm(f1, a_mid[...]) + mm(f1h[r].reshape(rows, 2 * BLK), a_bnd[...])
        mx[r, 2 * C :] = f2.astype(BF16).reshape(ct, C, S)
        tot = gm_acc[:, : 3 * C]
        for u in range(ct):
            t = ch * ct + u
            tot = tot + nt(co[t], mx[t])
        gm_acc[:, : 3 * C] = tot

    loop(n_ch, forward_two)

    def finish(ch):
        b, t0 = ch // per_b, lax.rem(ch, per_b) * ct
        r = pl.ds(ch * ct, ct)
        arrived(ex_c(1)(ch))
        gh[r, :, lo] = gh[r, :, lo] + recv_c[1, 0, r].astype(F32)
        gh[r, :, hi] = gh[r, :, hi] + recv_c[1, 1, r].astype(F32)
        tot = gc_acc[:, : 2 * C]
        tob = gb_acc[...]
        for u in range(ct):
            t = ch * ct + u
            g, f, s = gh[t], fb[t], sg[t]
            gs = g * s
            v = jnp.concatenate([gs * (1.0 - f * f), gs * f * (1.0 - s)], axis=0).astype(BF16)
            gp[b, t0 + u] = v
            w = v.astype(F32)
            for m in range(nb):
                tob = tob + w[:, m * BLK : (m + 1) * BLK]
            tot = tot + nt(v, xm[b, pl.ds(t0 + u, 2)].reshape(2 * C, S))
        gc_acc[:, : 2 * C] = tot
        gb_acc[...] = tob

    loop(n_ch, finish)

    pack[:, 16:24, :] = jnp.zeros((GROUP, 8, BLK), F32)
    lane = lax.broadcasted_iota(jnp.int32, (2 * C, BLK), 1)
    both = jnp.where(lane < 2 * C, gc_acc[...], jnp.sum(gb_acc[...], axis=1, keepdims=True))
    for i in range(GROUP):
        o = 8 * (i % 4)
        p = BLK * (i // 4)
        pack[i, 0:8] = gs_acc[o : o + 8, p : p + BLK]
        pack[i, 8:16] = both[8 * i : 8 * i + 8]
        pack[i, 16:20] = gm_acc[4 * i : 4 * i + 4]

    def rs(j):
        peer = lax.rem(loc + j, GROUP)
        return pltpu.make_async_remote_copy(
            src_ref=pack.at[peer], dst_ref=rs_buf.at[j], send_sem=r_send.at[j],
            recv_sem=r_recv.at[j], device_id={"site": base + peer}, device_id_type=MESH,
        )

    def cross(j):
        return pltpu.make_async_remote_copy(
            src_ref=dp_buf.at[q], dst_ref=dp_buf.at[q], send_sem=d_send.at[j],
            recv_sem=d_recv.at[j], device_id=cross_peer(j), device_id_type=MESH,
        )

    def gather(j):
        return pltpu.make_async_remote_copy(
            src_ref=got.at[loc], dst_ref=got.at[loc], send_sem=a_send.at[j],
            recv_sem=a_recv.at[j], device_id={"site": group_peer(j)}, device_id_type=MESH,
        )

    for j in range(1, GROUP):
        rs(j).start()

    wct_now, wct_old = wct[C:, :], wct[:C, :]

    def inputs_grad(ch):
        b, t0 = ch // per_b, lax.rem(ch, per_b) * ct
        for u in range(ct):
            v = mm(wct_now, gp[b, t0 + u]) + mm(wct_old, gp[b, t0 + u + 1])
            gi[b, t0 + u] = v.astype(BF16)

    loop(n_ch, inputs_grad)

    total = pack[loc]
    for j in range(1, GROUP):
        rs(j).wait_recv()
        total = total + rs_buf[j]
    dp_buf[q] = total
    for j in range(1, n_q):
        cross(j).start()
    for j in range(1, n_q):
        cross(j).wait_recv()
    total = dp_buf[0]
    for i in range(1, n_q):
        total = total + dp_buf[i]
    got[loc] = total
    for j in range(1, GROUP):
        gather(j).start()
    for j in range(1, GROUP):
        gather(j).wait_recv()

    fin[...] = got[...]

    for ch in range(n_ch):
        for make in (ex_x, ex_c(0), ex_c(1), ex_f):
            for p in make(ch):
                p.wait_send()
    for j in range(1, GROUP):
        rs(j).wait_send()
        gather(j).wait_send()
    for j in range(1, n_q):
        cross(j).wait_send()


def unpack(fin, gi, out_conv, out_bias, out_mix, out_skip, out_gi, sem):
    copy = pltpu.make_async_copy(gi, out_gi, sem)
    copy.start()
    n = out_conv.shape[0]
    c = out_mix.shape[0]
    for h in range(2):
        out_skip[:, h * BLK : (h + 1) * BLK] = fin[4 * h : 4 * h + 4, 0:8].reshape(c, BLK)
    both = fin[:, 8:16].reshape(n, BLK)
    out_conv[...] = both[:, :n]
    out_bias[...] = both.T[n : n + 1, :]
    for i in range(GROUP):
        out_mix[4 * i : 4 * i + 4, :] = fin[i, 16:20, : out_mix.shape[1]]
    copy.wait()


def pin(x):
    return pltpu.with_memory_space_constraint(x, pltpu.HBM)


def shards(mesh_shape, x, co, cs, wc, bias, wm, ws, cols, cnt, adj):
    n_site, n_dp = mesh_shape
    n_b, n_t, C, S = x.shape
    K = cols.shape[1]
    skip = cs.shape[2]
    ct = 6
    n_ch = n_b * n_t // ct
    n = n_b * n_t
    n_q = (n_site // GROUP) * n_dp
    cfg = (n_site, n_dp, n_b, n_t, C, S, K, ct)
    vm = pl.BlockSpec(memory_space=pltpu.VMEM)
    anys = pl.BlockSpec(memory_space=pltpu.HBM)
    V = pltpu.VMEM
    D = pltpu.SemaphoreType.DMA
    scratch = [
        V((n_b, n_t + 1, C, S), BF16),
        V((n_b, n_t + 1, C, 2 * BLK), BF16),
        V((n, C, S), BF16),
        V((n, skip, S), BF16),
        V(adj.shape, BF16),
        V((S, S), BF16),
        V((2 * BLK, S), BF16),
        V((2 * C, 2 * C), BF16),
        V((3 * C, C), BF16),
        V((2 * C, BLK), F32),
        V((n, C, S), BF16),
        V((n, C, S), F32),
        V((2, 2, n, C, BLK), BF16),
        V((2, 2, n, C, BLK), BF16),
        V((n, C, S), F32),
        V((n, C, S), F32),
        V((n, 3 * C, S), BF16),
        V((n, C, 2 * BLK), BF16),
        V((n, C, 2 * BLK), BF16),
        V((n, C, S), F32),
        V((n_b, n_t + 1, 2 * C, S), BF16),
        V((C, skip), F32),
        V((C, BLK), F32),
        V((2 * C, BLK), F32),
        V((2 * C, BLK), F32),
        V((GROUP, 24, BLK), F32),
        V((GROUP, 24, BLK), F32),
        V((n_q, 24, BLK), F32),
        V((GROUP, 24, BLK), F32),
        V((2 * C, 2 * C), BF16),
        V((1, 2 * C), F32),
        V((C, 3 * C), BF16),
        V((C, skip), BF16),
        pltpu.SMEM(cols.shape, jnp.int32),
        pltpu.SMEM(cnt.shape, jnp.int32),
        D((6,)),
        D((3,)),
        D((n_ch,)),
        D((4, 2, n_ch)),
        D((4, 2, n_ch)),
        D((GROUP,)),
        D((GROUP,)),
        D((n_q,)),
        D((n_q,)),
        D((GROUP,)),
        D((GROUP,)),
    ]
    fin, gi = pl.pallas_call(
        functools.partial(kernel, cfg),
        out_shape=(
            jax.ShapeDtypeStruct((GROUP, 24, BLK), F32),
            jax.ShapeDtypeStruct(x.shape, BF16),
        ),
        in_specs=[anys] * 10,
        out_specs=(vm, vm),
        scratch_shapes=scratch,
        compiler_params=pltpu.CompilerParams(
            collective_id=0, has_side_effects=True, vmem_limit_bytes=VMEM_LIMIT
        ),
        name="layer",
    )(
        *map(
            pin,
            (
                x, co.reshape(n, C, S), cs.reshape(n, skip, S), wc, bias.reshape(1, -1), wm, ws.T,
                cols, cnt, adj,
            ),
        )
    )
    conv, gb, mix, gskip, gin = pl.pallas_call(
        unpack,
        out_shape=(
            jax.ShapeDtypeStruct((2 * C, 2 * C), F32),
            jax.ShapeDtypeStruct((1, 2 * C), F32),
            jax.ShapeDtypeStruct((C, 3 * C), F32),
            jax.ShapeDtypeStruct((C, skip), F32),
            jax.ShapeDtypeStruct(x.shape, BF16),
        ),
        in_specs=[vm, vm],
        out_specs=(vm, vm, vm, vm, pl.BlockSpec(memory_space=pltpu.HBM)),
        scratch_shapes=[D],
        compiler_params=pltpu.CompilerParams(vmem_limit_bytes=4 * 1024 * 1024),
        name="results",
    )(fin, gi)
    return conv, gb.reshape(-1), mix, gskip.T, gin


def solution(mesh):
    placed = (
        P("dp", None, None, "site"),
        P("dp", None, None, "site"),
        P("dp", None, None, "site"),
        P(),
        P(),
        P(),
        P(),
        P("site", None),
        P("site"),
        P("site", None, None, None),
    )
    return jax.shard_map(
        functools.partial(shards, (mesh.shape["site"], mesh.shape["dp"])),
        mesh=mesh,
        in_specs=placed,
        out_specs=(P(), P(), P(), P(), P("dp", None, None, "site")),
        check_vma=False,
    )
```

```python
import functools

import jax
import jax.numpy as jnp
from jax import lax
from jax.experimental import pallas as pl
from jax.experimental.pallas import tpu as pltpu
from jax.sharding import PartitionSpec as P

BLK = 128
GROUP = 8
VMEM_LIMIT = 40 * 1024 * 1024
MESH = pl.DeviceIdType.MESH
F32 = jnp.float32
BF16 = jnp.bfloat16


def mm(a, b):
    return jnp.dot(a, b, preferred_element_type=F32)


def nt(a, b):
    return lax.dot_general(a, b, (((1,), (1,)), ((), ())), preferred_element_type=F32)


def loop(n, f):
    def step(i, carry):
        f(i)
        return carry

    lax.fori_loop(0, n, step, 0)


def kernel(
    cfg,
    x_ref, co_ref, cs_ref, wc_hbm, bias_hbm, wm_hbm, ws_hbm, cols_hbm, cnt_hbm, adj_ref,
    fin, gi,
    xm, xh, co, cs, av, a_mid, a_bnd, wct, wmt, bcol,
    g2, c1, send_c, recv_c, fb, sg, mx, hh, f1h, gh, gp,
    gs_acc, gm_acc, gc_acc, gb_acc,
    pack_a, rs_a, dp_a, got_a, pack_b, rs_b, dp_b, got_b,
    wc_ref, bias_ref, wm_ref, ws_ref, cols_ref, cnt_ref, sem_small,
    sem_loc, sem_cs, e_send, e_recv, r_send, r_recv, d_send, d_recv, a_send, a_recv,
):
    n_site, n_dp, n_b, n_t, C, S, K, ct = cfg
    per_b = n_t // ct
    n_ch = n_b * per_b
    rows = ct * C
    nb = S // BLK
    site = lax.axis_index("site")
    dp = lax.axis_index("dp")
    right = lax.rem(site + 1, n_site)
    left = lax.rem(site + n_site - 1, n_site)
    n_q = (n_site // GROUP) * n_dp
    base = (site // GROUP) * GROUP
    loc = lax.rem(site, GROUP)
    q = (site // GROUP) * n_dp + dp

    def group_peer(j):
        return base + lax.rem(loc + j, GROUP)

    def cross_peer(j):
        other = lax.rem(q + j, n_q)
        return {"site": (other // n_dp) * GROUP + loc, "dp": lax.rem(other, n_dp)}

    barrier = pltpu.get_barrier_semaphore()
    signals = 0
    if n_site > GROUP:
        for p in (left, right):
            pl.semaphore_signal(barrier, inc=1, device_id={"site": p}, device_id_type=MESH)
            signals += 1
    for j in range(1, GROUP):
        pl.semaphore_signal(barrier, inc=1, device_id={"site": group_peer(j)}, device_id_type=MESH)
        signals += 1
    for j in range(1, n_q):
        pl.semaphore_signal(barrier, inc=1, device_id=cross_peer(j), device_id_type=MESH)
        signals += 1

    small = [
        pltpu.make_async_copy(src, dst, sem_small.at[i])
        for i, (src, dst) in enumerate(
            (
                (cols_hbm, cols_ref), (cnt_hbm, cnt_ref), (wm_hbm, wm_ref), (wc_hbm, wc_ref),
                (bias_hbm, bias_ref), (ws_hbm, ws_ref),
            )
        )
    ]
    for cp in small:
        cp.start()
    ld_adj = pltpu.make_async_copy(adj_ref, av, sem_loc.at[0])
    ld_co = pltpu.make_async_copy(co_ref, co, sem_loc.at[1])
    ld_x = pltpu.make_async_copy(x_ref, xm.at[:, 1:], sem_loc.at[2])
    ld_adj.start()
    ld_co.start()
    ld_x.start()

    def ld_cs(ch):
        r = pl.ds(ch * ct, ct)
        return pltpu.make_async_copy(cs_ref.at[r], cs.at[r], sem_cs.at[ch])

    for ch in range(n_ch):
        ld_cs(ch).start()

    for cp in small:
        cp.wait()
    wct[...] = wc_ref[...].astype(F32).T.astype(BF16)
    wmt[...] = wm_ref[...].astype(F32).T.astype(BF16)
    bcol[...] = jnp.broadcast_to(bias_ref[...], (BLK, 2 * C)).T
    for b in range(n_b):
        xm[b, 0] = jnp.zeros((C, S), BF16)
        xh[b, 0] = jnp.zeros((C, 2 * BLK), BF16)
        gp[b, n_t] = jnp.zeros((2 * C, S), BF16)

    pl.semaphore_wait(barrier, signals)

    def remote(src, dst, e, side, ch, target):
        return pltpu.make_async_remote_copy(
            src_ref=src, dst_ref=dst, send_sem=e_send.at[e, side, ch],
            recv_sem=e_recv.at[e, side, ch], device_id={"site": target}, device_id_type=MESH,
        )

    lo, hi = pl.ds(0, BLK), pl.ds(S - BLK, BLK)
    h_lo, h_hi = pl.ds(0, BLK), pl.ds(BLK, BLK)

    def ex_x(ch):
        b, t0 = ch // per_b, lax.rem(ch, per_b) * ct
        src = x_ref.at[b, pl.ds(t0, ct)]
        dst = xh.at[b, pl.ds(t0 + 1, ct)]
        return (
            remote(src.at[:, :, hi], dst.at[:, :, h_lo], 0, 0, ch, right),
            remote(src.at[:, :, lo], dst.at[:, :, h_hi], 0, 1, ch, left),
        )

    def ex_c(which):
        def make(ch):
            r = pl.ds(ch * ct, ct)
            return (
                remote(send_c.at[which, 1, r], recv_c.at[which, 0, r], 1 + which, 0, ch, right),
                remote(send_c.at[which, 0, r], recv_c.at[which, 1, r], 1 + which, 1, ch, left),
            )

        return make

    def ex_f(ch):
        r = pl.ds(ch * ct, ct)
        src = mx.at[r, pl.ds(C, C)]
        dst = f1h.at[r]
        return (
            remote(src.at[:, :, hi], dst.at[:, :, h_lo], 3, 0, ch, right),
            remote(src.at[:, :, lo], dst.at[:, :, h_hi], 3, 1, ch, left),
        )

    def start(pair):
        for p in pair:
            p.start()

    def arrived(pair):
        for p in pair:
            p.wait_recv()

    def sums(w, pack, rs_buf, dp_buf, got):
        def rs(j):
            peer = lax.rem(loc + j, GROUP)
            return pltpu.make_async_remote_copy(
                src_ref=pack.at[peer], dst_ref=rs_buf.at[j], send_sem=r_send.at[w, j],
                recv_sem=r_recv.at[w, j], device_id={"site": base + peer}, device_id_type=MESH,
            )

        def cross(j):
            return pltpu.make_async_remote_copy(
                src_ref=dp_buf.at[q], dst_ref=dp_buf.at[q], send_sem=d_send.at[w, j],
                recv_sem=d_recv.at[w, j], device_id=cross_peer(j), device_id_type=MESH,
            )

        def gather(j):
            return pltpu.make_async_remote_copy(
                src_ref=got.at[loc], dst_ref=got.at[loc], send_sem=a_send.at[w, j],
                recv_sem=a_recv.at[w, j], device_id={"site": group_peer(j)}, device_id_type=MESH,
            )

        return rs, cross, gather, pack, rs_buf, dp_buf, got

    def scatter(z):
        for j in range(1, GROUP):
            z[0](j).start()

    def exchange(z):
        rs, cross, gather, pack, rs_buf, dp_buf, got = z
        total = pack[loc]
        for j in range(1, GROUP):
            rs(j).wait_recv()
            total = total + rs_buf[j]
        dp_buf[q] = total
        for j in range(1, n_q):
            cross(j).start()

    def spread(z):
        rs, cross, gather, pack, rs_buf, dp_buf, got = z
        for j in range(1, n_q):
            cross(j).wait_recv()
        total = dp_buf[0]
        for i in range(1, n_q):
            total = total + dp_buf[i]
        got[loc] = total
        for j in range(1, GROUP):
            gather(j).start()

    def collect(z):
        for j in range(1, GROUP):
            z[2](j).wait_recv()

    for ch in range(n_ch):
        start(ex_x(ch))

    ld_adj.wait()
    for c in range(nb + 2):
        for r in range(nb):
            acc = jnp.zeros((BLK, BLK), F32)
            for k in range(K):
                on = jnp.where(
                    jnp.logical_and(cols_ref[r, k] == c, k < cnt_ref[r]), F32(1.0), F32(0.0)
                )
                acc = acc + av[r, k].astype(F32) * on
            blk = acc.astype(BF16)
            if c == 0 or c == nb + 1:
                o = 0 if c == 0 else BLK
                a_bnd[o : o + BLK, r * BLK : (r + 1) * BLK] = blk
            else:
                a_mid[(c - 1) * BLK : c * BLK, r * BLK : (r + 1) * BLK] = blk

    ld_co.wait()

    def back_one(ch):
        r = pl.ds(ch * ct, ct)
        for u in range(ct):
            t = ch * ct + u
            bm = mm(wmt[C:, :], co[t])
            c1[t] = bm[:C]
            g2[t] = bm[C:].astype(BF16)
        g = g2[r].reshape(rows, S)
        edge = nt(g, a_bnd[...]).astype(BF16).reshape(ct, C, 2 * BLK)
        send_c[0, 0, r] = edge[:, :, :BLK]
        send_c[0, 1, r] = edge[:, :, BLK:]
        start(ex_c(0)(ch))
        c1[r] = c1[r] + nt(g, a_mid[...]).reshape(ct, C, S)

    loop(n_ch, back_one)

    ld_x.wait()

    def forward_one(ch):
        b, t0 = ch // per_b, lax.rem(ch, per_b) * ct
        r = pl.ds(ch * ct, ct)
        arrived(ex_x(ch))
        for u in range(ct):
            t = ch * ct + u
            for src, width in ((xm, S), (xh, 2 * BLK)):
                st = src[b, pl.ds(t0 + u, 2)].reshape(2 * C, width)
                pre = mm(wc_ref[...], st) + bcol[:, 0:1]
                f = jnp.tanh(pre[:C])
                s = 0.5 * jnp.tanh(0.5 * pre[C:]) + 0.5
                h = (f * s).astype(BF16)
                if src is xm:
                    fb[t] = f
                    sg[t] = s
                    mx[t, 0:C] = h
                else:
                    hh[t] = h
        a = mx[r, 0:C].reshape(rows, S)
        f1 = mm(a, a_mid[...]) + mm(hh[r].reshape(rows, 2 * BLK), a_bnd[...])
        mx[r, C : 2 * C] = f1.astype(BF16).reshape(ct, C, S)
        start(ex_f(ch))

    loop(n_ch, forward_one)

    def back_two(ch):
        r = pl.ds(ch * ct, ct)
        arrived(ex_c(0)(ch))
        c1[r, :, lo] = c1[r, :, lo] + recv_c[0, 0, r].astype(F32)
        c1[r, :, hi] = c1[r, :, hi] + recv_c[0, 1, r].astype(F32)
        g = c1[r].astype(BF16).reshape(rows, S)
        edge = nt(g, a_bnd[...]).astype(BF16).reshape(ct, C, 2 * BLK)
        send_c[1, 0, r] = edge[:, :, :BLK]
        send_c[1, 1, r] = edge[:, :, BLK:]
        start(ex_c(1)(ch))
        gh[r] = nt(g, a_mid[...]).reshape(ct, C, S)

    loop(n_ch, back_two)

    gs_acc[...] = jnp.zeros_like(gs_acc)
    gm_acc[...] = jnp.zeros_like(gm_acc)
    gc_acc[...] = jnp.zeros_like(gc_acc)
    gb_acc[...] = jnp.zeros_like(gb_acc)

    def skip(ch):
        ld_cs(ch).wait()
        tot = gs_acc[...]
        for u in range(ct):
            t = ch * ct + u
            tot = tot + nt(mx[t, 0:C], cs[t])
            gh[t] = gh[t] + mm(ws_ref[...], cs[t]) + mm(wmt[:C, :], co[t])
        gs_acc[...] = tot

    loop(n_ch, skip)

    def forward_two(ch):
        r = pl.ds(ch * ct, ct)
        arrived(ex_f(ch))
        f1 = mx[r, C : 2 * C].reshape(rows, S)
        f2 = mm(f1, a_mid[...]) + mm(f1h[r].reshape(rows, 2 * BLK), a_bnd[...])
        mx[r, 2 * C :] = f2.astype(BF16).reshape(ct, C, S)
        tot = gm_acc[:, : 3 * C]
        for u in range(ct):
            t = ch * ct + u
            tot = tot + nt(co[t], mx[t])
        gm_acc[:, : 3 * C] = tot

    loop(n_ch, forward_two)

    pack_a[:, 8:16, :] = jnp.zeros((GROUP, 8, BLK), F32)
    for i in range(GROUP):
        o = 8 * (i % 4)
        p = BLK * (i // 4)
        pack_a[i, 0:8] = gs_acc[o : o + 8, p : p + BLK]
        pack_a[i, 8:12] = gm_acc[4 * i : 4 * i + 4]
    early = sums(0, pack_a, rs_a, dp_a, got_a)
    scatter(early)

    def finish(ch):
        b, t0 = ch // per_b, lax.rem(ch, per_b) * ct
        r = pl.ds(ch * ct, ct)
        arrived(ex_c(1)(ch))
        gh[r, :, lo] = gh[r, :, lo] + recv_c[1, 0, r].astype(F32)
        gh[r, :, hi] = gh[r, :, hi] + recv_c[1, 1, r].astype(F32)
        tot = gc_acc[:, : 2 * C]
        tob = gb_acc[...]
        for u in range(ct):
            t = ch * ct + u
            g, f, s = gh[t], fb[t], sg[t]
            gs = g * s
            v = jnp.concatenate([gs * (1.0 - f * f), gs * f * (1.0 - s)], axis=0).astype(BF16)
            gp[b, t0 + u] = v
            w = v.astype(F32)
            for m in range(nb):
                tob = tob + w[:, m * BLK : (m + 1) * BLK]
            tot = tot + nt(v, xm[b, pl.ds(t0 + u, 2)].reshape(2 * C, S))
        gc_acc[:, : 2 * C] = tot
        gb_acc[...] = tob

    loop(n_ch, finish)

    lane = lax.broadcasted_iota(jnp.int32, (2 * C, BLK), 1)
    both = jnp.where(lane < 2 * C, gc_acc[...], jnp.sum(gb_acc[...], axis=1, keepdims=True))
    for i in range(GROUP):
        pack_b[i] = both[8 * i : 8 * i + 8]
    late = sums(1, pack_b, rs_b, dp_b, got_b)
    scatter(late)
    exchange(early)

    wct_now, wct_old = wct[C:, :], wct[:C, :]

    def inputs_grad(ch):
        b, t0 = ch // per_b, lax.rem(ch, per_b) * ct
        for u in range(ct):
            v = mm(wct_now, gp[b, t0 + u]) + mm(wct_old, gp[b, t0 + u + 1])
            gi[b, t0 + u] = v.astype(BF16)

    loop(n_ch, inputs_grad)

    exchange(late)
    spread(early)
    spread(late)
    collect(early)
    collect(late)

    fin[:, 0:8, :] = got_a[:, 0:8, :]
    fin[:, 8:16, :] = got_b[...]
    fin[:, 16:24, :] = got_a[:, 8:16, :]

    for ch in range(n_ch):
        for make in (ex_x, ex_c(0), ex_c(1), ex_f):
            for p in make(ch):
                p.wait_send()
    for z in (early, late):
        for j in range(1, GROUP):
            z[0](j).wait_send()
            z[2](j).wait_send()
        for j in range(1, n_q):
            z[1](j).wait_send()


def unpack(fin, gi, out_conv, out_bias, out_mix, out_skip, out_gi, sem):
    copy = pltpu.make_async_copy(gi, out_gi, sem)
    copy.start()
    n = out_conv.shape[0]
    c = out_mix.shape[0]
    for h in range(2):
        out_skip[:, h * BLK : (h + 1) * BLK] = fin[4 * h : 4 * h + 4, 0:8].reshape(c, BLK)
    both = fin[:, 8:16].reshape(n, BLK)
    out_conv[...] = both[:, :n]
    out_bias[...] = both.T[n : n + 1, :]
    for i in range(GROUP):
        out_mix[4 * i : 4 * i + 4, :] = fin[i, 16:20, : out_mix.shape[1]]
    copy.wait()


def pin(x):
    return pltpu.with_memory_space_constraint(x, pltpu.HBM)


def shards(mesh_shape, x, co, cs, wc, bias, wm, ws, cols, cnt, adj):
    n_site, n_dp = mesh_shape
    n_b, n_t, C, S = x.shape
    K = cols.shape[1]
    skip = cs.shape[2]
    ct = 12
    n_ch = n_b * n_t // ct
    n = n_b * n_t
    n_q = (n_site // GROUP) * n_dp
    cfg = (n_site, n_dp, n_b, n_t, C, S, K, ct)
    vm = pl.BlockSpec(memory_space=pltpu.VMEM)
    anys = pl.BlockSpec(memory_space=pltpu.HBM)
    V = pltpu.VMEM
    D = pltpu.SemaphoreType.DMA
    scratch = [
        V((n_b, n_t + 1, C, S), BF16),
        V((n_b, n_t + 1, C, 2 * BLK), BF16),
        V((n, C, S), BF16),
        V((n, skip, S), BF16),
        V(adj.shape, BF16),
        V((S, S), BF16),
        V((2 * BLK, S), BF16),
        V((2 * C, 2 * C), BF16),
        V((3 * C, C), BF16),
        V((2 * C, BLK), F32),
        V((n, C, S), BF16),
        V((n, C, S), F32),
        V((2, 2, n, C, BLK), BF16),
        V((2, 2, n, C, BLK), BF16),
        V((n, C, S), F32),
        V((n, C, S), F32),
        V((n, 3 * C, S), BF16),
        V((n, C, 2 * BLK), BF16),
        V((n, C, 2 * BLK), BF16),
        V((n, C, S), F32),
        V((n_b, n_t + 1, 2 * C, S), BF16),
        V((C, skip), F32),
        V((C, BLK), F32),
        V((2 * C, BLK), F32),
        V((2 * C, BLK), F32),
        V((GROUP, 16, BLK), F32),
        V((GROUP, 16, BLK), F32),
        V((n_q, 16, BLK), F32),
        V((GROUP, 16, BLK), F32),
        V((GROUP, 8, BLK), F32),
        V((GROUP, 8, BLK), F32),
        V((n_q, 8, BLK), F32),
        V((GROUP, 8, BLK), F32),
        V((2 * C, 2 * C), BF16),
        V((1, 2 * C), F32),
        V((C, 3 * C), BF16),
        V((C, skip), BF16),
        pltpu.SMEM(cols.shape, jnp.int32),
        pltpu.SMEM(cnt.shape, jnp.int32),
        D((6,)),
        D((3,)),
        D((n_ch,)),
        D((4, 2, n_ch)),
        D((4, 2, n_ch)),
        D((2, GROUP)),
        D((2, GROUP)),
        D((2, n_q)),
        D((2, n_q)),
        D((2, GROUP)),
        D((2, GROUP)),
    ]
    fin, gi = pl.pallas_call(
        functools.partial(kernel, cfg),
        out_shape=(
            jax.ShapeDtypeStruct((GROUP, 24, BLK), F32),
            jax.ShapeDtypeStruct(x.shape, BF16),
        ),
        in_specs=[anys] * 10,
        out_specs=(vm, vm),
        scratch_shapes=scratch,
        compiler_params=pltpu.CompilerParams(
            collective_id=0, has_side_effects=True, vmem_limit_bytes=VMEM_LIMIT
        ),
        name="layer",
    )(
        *map(
            pin,
            (
                x, co.reshape(n, C, S), cs.reshape(n, skip, S), wc, bias.reshape(1, -1), wm, ws.T,
                cols, cnt, adj,
            ),
        )
    )
    conv, gb, mix, gskip, gin = pl.pallas_call(
        unpack,
        out_shape=(
            jax.ShapeDtypeStruct((2 * C, 2 * C), F32),
            jax.ShapeDtypeStruct((1, 2 * C), F32),
            jax.ShapeDtypeStruct((C, 3 * C), F32),
            jax.ShapeDtypeStruct((C, skip), F32),
            jax.ShapeDtypeStruct(x.shape, BF16),
        ),
        in_specs=[vm, vm],
        out_specs=(vm, vm, vm, vm, pl.BlockSpec(memory_space=pltpu.HBM)),
        scratch_shapes=[D],
        compiler_params=pltpu.CompilerParams(vmem_limit_bytes=4 * 1024 * 1024),
        name="results",
    )(fin, gi)
    return conv, gb.reshape(-1), mix, gskip.T, gin


def solution(mesh):
    placed = (
        P("dp", None, None, "site"),
        P("dp", None, None, "site"),
        P("dp", None, None, "site"),
        P(),
        P(),
        P(),
        P(),
        P("site", None),
        P("site"),
        P("site", None, None, None),
    )
    return jax.shard_map(
        functools.partial(shards, (mesh.shape["site"], mesh.shape["dp"])),
        mesh=mesh,
        in_specs=placed,
        out_specs=(P(), P(), P(), P(), P("dp", None, None, "site")),
        check_vma=False,
    )
```
